32 devices in a mesh: row: 8 (over z, x), col: 4 (over y, core).
Axes of the slice: x: 2, y: 2, z: 4, core: 2. Of those that a mesh axis runs over, the one named last changes fastest.
Arguments:
- points: bfloat16 [48, 1024, 1024], P('row', 'col')
- targets: bfloat16 [48, 1024, 1000], P('row', 'col'), may hold values from -6 to 6
- coeffs: float32 [48, 1024, 1000], P('row', 'col'), may hold values from -0.375 to 0.375
- block_inverse: float32 [48, 1024, 1024], P('row', 'col'), as said below
- block_order: int32 [48], replicated, may hold values from 0 to 47, each once
Outputs:
- coeffs_out: float32 [48, 1024, 1000], P('row', 'col')
The draws below stay inside these ranges and needn't reach their ends.
Inputs may be any that keep to these rules, and one draw needn't show every extreme that they name: block_inverse[b] is the float32 inverse of the exact Gaussian kernel matrix of block b's points (as in the reference program) plus the identity.
All inputs are finite; a program needn't handle non-finite values.
Results may differ from the reference program's by a relative error of at most 0.0003.
Values may be sent and summed in bfloat16 or wider, within the bound.
No kernel may reach another device: no remote copies, remote signals or barrier semaphores. Data moves between devices by JAX's collectives and lax.ppermute only.
A program may use at most 128 MiB of HBM per device.

```python
import jax
import jax.numpy as jnp
from jax import lax

F = 1024
C = 1000
BS = 1024
STEPS = 2
NB = 48


latent_width = 16


ridge_weight = 1.0


def make_points(key):
    latent = jax.random.normal(jax.random.fold_in(key, 11), (NB, BS, latent_width), jnp.float32)
    mixing = jax.random.normal(jax.random.fold_in(key, 12), (latent_width, F), jnp.float32)
    noise = 1.0 * jax.random.normal(jax.random.fold_in(key, 13), (NB, BS, F), jnp.float32)
    return (0.25 * jnp.einsum('nbl,lf->nbf', latent, mixing) + noise).astype(jnp.bfloat16)


def draw_points(key, part):
    return make_points(key)


def draw_block_inverse(key, part):
    rounded = make_points(key).astype(jnp.float32)

    def invert(block_points):
        squares = jnp.sum(block_points * block_points, axis=1)
        inner = jnp.dot(block_points, block_points.T, precision=lax.Precision.HIGHEST)
        distance = squares[:, None] + squares[None, :] - 2.0 * inner
        kernel = jnp.exp(-distance * (0.5 / F))
        return jnp.linalg.inv(kernel + ridge_weight * jnp.eye(BS, dtype=jnp.float32))
    return lax.map(invert, rounded)


def level_of(own_key, shape, split, low, top_value):
    def one(position, parts):
        steps = jax.random.uniform(jax.random.fold_in(jax.random.fold_in(own_key, 6), position), (parts,), jnp.float32, low / len(split), top_value / len(split))
        return jnp.repeat(jnp.exp(steps), shape[position] // parts).reshape((-1,) + (1,) * (len(shape) - position - 1))

    gain = one(*split[0])
    for cut in split[1:]:
        gain = gain * one(*cut)
    return gain


def gaussian(key, extent, width, limit, pieces=(), held_as=jnp.bfloat16):
    factor_of = level_of(key, extent, pieces, -0.22, 0.18) if pieces else 1.0
    values = jax.random.normal(key, extent, jnp.float32) * width * factor_of
    return jnp.minimum(jnp.maximum(values, -limit), limit).astype(held_as)


def setup_inputs(seed: int = 0) -> dict:
    seeds = jax.random.split(jax.random.key(seed), 6)
    return {
        "points": draw_points(jax.random.fold_in(seeds[5], 71), 0),
        "targets": gaussian(seeds[1], (NB, BS, C), 1.0, 6.0, ((0, 8), (1, 4))),
        "coeffs": gaussian(seeds[2], (NB, BS, C), (6.0 / (NB * BS) ** 0.5), 0.375, ((0, 8), (1, 4)), jnp.float32),
        "block_inverse": draw_block_inverse(jax.random.fold_in(seeds[5], 71), 0),
        "block_order": jax.random.permutation(seeds[4], NB).astype(jnp.int32),
    }


ridge_weight = 1.0

def kernel_tile(left_points, right_points):
    left_wide = left_points.astype(jnp.float32)
    right_wide = right_points.astype(jnp.float32)
    inner = lax.dot_general(left_points.astype(jnp.float32), right_points.astype(jnp.float32), (((1,), (1,)), ((), ())), preferred_element_type=jnp.float32)
    distance = jnp.sum(left_wide * left_wide, axis=1)[:, None] + jnp.sum(right_wide * right_wide, axis=1)[None, :] - 2.0 * inner
    return jnp.exp(-distance * (0.5 / left_points.shape[1]))

def reference(points, targets, coeffs, block_inverse, block_order):
    current = coeffs
    for sweep_step in range(STEPS):
        block_id = block_order[sweep_step].astype(jnp.int32)
        active = lax.dynamic_index_in_dim(points, block_id, 0, keepdims=False)

        def accumulate(summed, block_pair):
            other_points, other_coeffs = block_pair
            return (summed + jnp.dot(kernel_tile(active, other_points).astype(jnp.float32), other_coeffs.astype(jnp.float32), precision=lax.Precision.HIGHEST, preferred_element_type=jnp.float32), None)
        summed, unused = lax.scan(accumulate, jnp.zeros((BS, C), jnp.float32), (points, current))
        previous = lax.dynamic_index_in_dim(current, block_id, 0, keepdims=False)
        wanted = lax.dynamic_index_in_dim(targets, block_id, 0, keepdims=False).astype(jnp.float32)
        residual = wanted - summed - ridge_weight * previous
        inverse_block = lax.dynamic_index_in_dim(block_inverse, block_id, 0, keepdims=False)
        refreshed = previous + jnp.dot(inverse_block.astype(jnp.float32), residual.astype(jnp.float32), precision=lax.Precision.HIGHEST, preferred_element_type=jnp.float32)
        current = lax.dynamic_update_index_in_dim(current, refreshed, block_id, 0)
    return current
```

```python
import functools

import jax
import jax.numpy as jnp
from jax import lax
from jax.experimental import pallas as pl
from jax.experimental.pallas import tpu as pltpu
from jax.sharding import PartitionSpec as P

STEPS = 2

AHEAD = 2

ridge_weight = 1.0

HIGH = lax.Precision.HIGH


def bits_of(count):
    if count & (count - 1):
        raise ValueError("not a power")
    return count.bit_length() - 1


def my_bit(bit):
    axis, place = bit
    return (lax.axis_index(axis) >> place) & 1


def swap(value, bit, sizes):
    axis, place = bit
    pairs = [(i, i ^ (1 << place)) for i in range(sizes[axis])]
    return lax.ppermute(value, axis, pairs)


def pick(value, index, dim):
    return lax.dynamic_index_in_dim(value, index, dim, keepdims=False)


LANES = 128
TOP = 32767.0
OCTAVE = 64.0


def scale_of(value, dim):
    top = jnp.max(jnp.abs(value), axis=dim, keepdims=True)
    return jnp.clip(jnp.ceil(jnp.log2(top) * OCTAVE), -100.0 * OCTAVE, 100.0 * OCTAVE)


def rounded(value, power):
    scaled = jnp.round(value * (jnp.exp2(power * (-1.0 / OCTAVE)) * TOP))
    return jnp.clip(scaled, -TOP, TOP).astype(jnp.int16)


def restored(codes, power):
    scale = jnp.exp2(power.astype(jnp.float32) * (1.0 / OCTAVE)) * (1.0 / TOP)
    return codes.astype(jnp.float32) * scale


def encode(value):
    power = scale_of(value, -1)
    extra = jnp.broadcast_to(power.astype(jnp.int16), value.shape[:-1] + (LANES,))
    return jnp.concatenate([rounded(value, power), extra], axis=-1)


def decode(codes):
    return restored(codes[..., :-LANES], codes[..., -LANES:][..., :1])


def natural(value, done, lead, sizes):
    order = sorted(done, key=lambda b: (b[0] == "row", -b[1]))
    perm = list(range(lead)) + [lead + done.index(b) for b in order]
    perm += list(range(lead + len(done), value.ndim))
    return value.transpose(perm)


def kernel_of(left, left_squares, right, right_squares):
    inner = lax.dot_general(
        left, right, (((1,), (1,)), ((), ())), preferred_element_type=jnp.float32
    )
    distance = left_squares[:, None] + right_squares[None, :] - 2.0 * inner
    return jnp.exp(-distance * (0.5 / left.shape[1]))


def squares_of(points):
    wide = points.astype(jnp.float32)
    return jnp.sum(wide * wide, axis=1)


def tile_of(points, active, active_squares):
    features = points.shape[-1]
    inner = lax.dot_general(points, active, (((1,), (1,)), ((), ())), preferred_element_type=jnp.float32)
    wide = points.astype(jnp.float32)
    squares = jnp.sum(wide * wide, axis=1, keepdims=True)
    distance = squares + active_squares - 2.0 * inner
    return jnp.exp(-distance * (0.5 / features))

def split(value):
    top = value.astype(jnp.bfloat16)
    return top, (value - top.astype(jnp.float32)).astype(jnp.bfloat16)

def partial_kernel(
    part, place_ref, points_ref, active_ref, coeffs_ref, previous_ref, wanted_ref, *rest
):
    out_ref, high, low, left_high, left_low = rest[-5:]
    blocks_here, per_col, features = points_ref.shape
    columns = active_ref.shape[0]

    @pl.when(pl.program_id(0) == 0)
    def _():
        wide = active_ref[...].astype(jnp.float32)
        ones = jnp.ones((8, features), jnp.bfloat16)
        active_squares = sum(
            lax.dot_general(
                ones, piece, (((1,), (1,)), ((), ())), preferred_element_type=jnp.float32
            )
            for piece in split(wide * wide)
        )[:1]
        for block in range(blocks_here):
            rows = pl.ds(block * per_col, per_col)
            tile = tile_of(points_ref[block], active_ref[...], active_squares)
            high[rows], low[rows] = split(tile)

    for block in range(blocks_here):
        lanes = pl.ds(block * per_col, per_col)
        left_high[:, lanes], left_low[:, lanes] = split(coeffs_ref[block])
    total = jnp.dot(left_high[...], high[...], preferred_element_type=jnp.float32)
    total += jnp.dot(left_high[...], low[...], preferred_element_type=jnp.float32)
    total += jnp.dot(left_low[...], high[...], preferred_element_type=jnp.float32)
    own = ridge_weight * previous_ref[0] - wanted_ref[0].astype(jnp.float32)
    own = jnp.concatenate([own] * (columns // per_col), axis=1)
    lane = lax.broadcasted_iota(jnp.int32, own.shape, 1) + part * columns
    first = place_ref[1]
    mine = (lane >= first) & (lane < first + per_col)
    out_ref[...] = total + jnp.where(mine, own, 0.0)


def partial_sum(place, points, active, coeffs, wanted, padded, part, parts, base):
    blocks_here, per_col, features = points.shape
    block_size = active.shape[0]
    columns = block_size // parts
    steps = 4
    tile = padded // steps
    held = pltpu.VMEM((blocks_here * per_col, columns), jnp.bfloat16)
    left = pltpu.VMEM((tile, blocks_here * per_col), jnp.bfloat16)
    specs = [
        pl.BlockSpec(points.shape, lambda i, place: (0, 0, 0)),
        pl.BlockSpec((columns, features), lambda i, place: (part, 0)),
        pl.BlockSpec((blocks_here, tile, per_col), lambda i, place: (0, i, 0)),
        pl.BlockSpec((1, tile, per_col), lambda i, place: (place[0], i, 0)),
        pl.BlockSpec((1, tile, per_col), lambda i, place: (place[0], i, 0)),
    ]
    given = [place, points, active, coeffs, coeffs, wanted]
    aliases = {}
    if base is not None:
        specs.append(pl.BlockSpec(memory_space=pl.ANY))
        aliases = {len(given): 0}
        given.append(base)
    return pl.pallas_call(
        functools.partial(partial_kernel, part),
        grid_spec=pltpu.PrefetchScalarGridSpec(
            num_scalar_prefetch=1,
            grid=(steps,),
            in_specs=specs,
            out_specs=pl.BlockSpec((tile, columns), lambda i, place: (i, part)),
            scratch_shapes=[held, held, left, left],
        ),
        out_shape=jax.ShapeDtypeStruct((padded, block_size), jnp.float32),
        input_output_aliases=aliases,
        cost_estimate=pl.CostEstimate(
            flops=2 * blocks_here * per_col * columns * (features + 3 * padded),
            transcendentals=blocks_here * per_col * columns,
            bytes_accessed=12 << 20,
        ),
    )(*given)


def scatter(value, owner, places):
    for place in places:
        mine = my_bit(("row", place))
        kept, sent = pick(value, mine, 0), pick(value, 1 - mine, 0)
        (got,), _ = yield [(sent, ("row", place))], []
        value = jnp.where(((owner >> place) & 1) == mine, kept, got)
    return value


def cut_rows(value, row_bits, places):
    value = value.reshape((2,) * row_bits + (value.shape[0] >> row_bits,) + value.shape[1:])
    order = [row_bits - 1 - place for place in places]
    return value.transpose(order + list(range(row_bits, value.ndim)))


def joined(value, got, bit, dim):
    first = my_bit(bit) == 0
    return jnp.stack([jnp.where(first, value, got), jnp.where(first, got, value)], axis=dim)


def gather(value, bits, done):
    for bit in bits:
        (got,), _ = yield [(value, bit)], []
        value = joined(value, got, bit, 0)
        done.insert(0, bit)
    return value


class Plan:
    def __init__(self, sizes, shape, classes):
        self.blocks_here, self.per_col, self.features = shape
        self.rows, self.cols = sizes["row"], sizes["col"]
        row_bits, col_bits = bits_of(self.rows), bits_of(self.cols)
        self.row_bits, self.col_bits = row_bits, col_bits
        self.block_size = self.per_col * self.cols
        devices = self.rows * self.cols
        chunk = -(-classes // devices)
        self.chunk = chunk + chunk % 2
        self.padded = self.chunk * devices
        self.classes = classes
        self.high_first = list(range(row_bits - 1, 0, -1))
        self.low_first = self.high_first[::-1]
        self.near = ("row", 0)
        self.wide = ("col", col_bits - 1)
        self.col_rest = [("col", p) for p in range(col_bits - 2, -1, -1)]
        self.scatter_order = [0] + self.high_first
        self.gather_order = [("row", p) for p in self.low_first + [0]]


def points_task(plan, own_points, owner):
    value = cut_rows(own_points, plan.row_bits, plan.scatter_order)
    value = yield from scatter(value, owner, plan.scatter_order)
    done = []
    value = yield from gather(value, [("row", p) for p in plan.low_first], done)
    half = value.shape[-2] // 2
    parts = [value[..., :half, :], value[..., half:, :]]
    dones = [list(done), list(done)]
    orders = ((plan.near, plan.wide), (plan.wide, plan.near))
    for step in range(2):
        bits = [order[step] for order in orders]
        got, _ = yield list(zip(parts, bits)), []
        parts = [joined(p, g, b, 0) for p, g, b in zip(parts, got, bits)]
        for d, b in zip(dones, bits):
            d.insert(0, b)
    parts = [natural(p, d, 0, None) for p, d in zip(parts, dones)]
    value = jnp.concatenate(parts, axis=-2)
    done = sorted(dones[0], key=lambda b: (b[0] == "row", -b[1]))
    value = yield from gather(value, plan.col_rest, done)
    value = natural(value, done, 0, None)
    return value.reshape(plan.block_size, plan.features)


def inverse_codes(plan, own_rows):
    block_size = plan.block_size
    on_diagonal = diagonal_of(plan, own_rows.shape)
    diagonal = jnp.sum(jnp.where(on_diagonal, own_rows, 0.0), axis=-1, keepdims=True)
    codes = encode(jnp.where(on_diagonal, 0.0, own_rows))
    first = jnp.round(diagonal * 16384.0)
    second = jnp.round((diagonal * 16384.0 - first) * 32768.0)
    lane = lax.broadcasted_iota(jnp.int32, codes.shape, codes.ndim - 1) - block_size
    codes = jnp.where(lane == 1, first.astype(jnp.int16), codes)
    return jnp.where(lane == 2, second.astype(jnp.int16), codes)


def diagonal_of(plan, shape):
    i = lax.broadcasted_iota(jnp.int32, shape, len(shape) - 2)
    j = lax.broadcasted_iota(jnp.int32, shape, len(shape) - 1)
    return j == i + lax.axis_index("col") * plan.per_col


def inverse_task(plan, values, owners):
    values = [cut_rows(v, plan.row_bits, plan.scatter_order) for v in values]
    for place in plan.scatter_order:
        mine = my_bit(("row", place))
        sent = jnp.stack([pick(v, 1 - mine, 0) for v in values])
        (got,), _ = yield [(sent, ("row", place))], []
        values = [
            jnp.where(((owner >> place) & 1) == mine, pick(v, mine, 0), g)
            for v, g, owner in zip(values, got, owners)
        ]
    value = jnp.stack(values, axis=-3)
    done = []
    for bit in plan.gather_order:
        (got,), _ = yield [(value, bit)], []
        value = joined(value, got, bit, 0)
        done.insert(0, bit)
    value = jnp.moveaxis(natural(value, done, 0, None), -3, 0)
    return value.reshape(len(values), plan.per_col, -1)


def inverse_of(plan, codes):
    block_size = plan.block_size
    first = codes[:, block_size + 1 : block_size + 2].astype(jnp.float32)
    second = codes[:, block_size + 2 : block_size + 3].astype(jnp.float32)
    diagonal = first * (1.0 / 16384.0) + second * (1.0 / (16384.0 * 32768.0))
    whole = decode(codes)
    return jnp.where(diagonal_of(plan, whole.shape), diagonal, whole)


def reduce_task(plan, part):
    chunk, block_size = plan.chunk, plan.block_size
    part = part.reshape((2,) * (plan.row_bits + plan.col_bits) + (chunk, block_size))
    left = [("row", p) for p in range(plan.row_bits - 1, -1, -1)]
    left += [("col", p) for p in range(plan.col_bits - 1, -1, -1)]

    def halves(value, bit, left):
        dim, mine = left.index(bit), my_bit(bit)
        return pick(value, mine, dim), pick(value, 1 - mine, dim)

    for bit in plan.col_rest[::-1]:
        kept, sent = halves(part, bit, left)
        (got,), _ = yield [(sent, bit)], []
        part = kept + got
        left.remove(bit)
    half = chunk // 2
    pieces = [part[..., :half, :], part[..., half:, :]]
    lefts = [list(left), list(left)]
    orders = ((plan.near, plan.wide), (plan.wide, plan.near))
    for step in range(2):
        bits = [order[step] for order in orders]
        pairs = [halves(p, b, l) for p, b, l in zip(pieces, bits, lefts)]
        got, _ = yield [(sent, b) for (_, sent), b in zip(pairs, bits)], []
        pieces = [kept + g for (kept, _), g in zip(pairs, got)]
        for l, b in zip(lefts, bits):
            l.remove(b)
    part = jnp.concatenate(pieces, axis=-2)
    left = lefts[0]
    for place in plan.high_first:
        bit = ("row", place)
        kept, sent = halves(part, bit, left)
        (got,), _ = yield [(sent, bit)], []
        part = kept + got
        left.remove(bit)
    done = []
    part = yield from gather(part, [plan.wide] + plan.col_rest, done)
    return natural(part, done, 0, None).reshape(plan.cols * chunk, block_size)


def change_of(plan, wrong, inverse):
    change = -lax.dot_general(
        wrong,
        inverse,
        (((1,), (1,)), ((), ())),
        precision=HIGH,
        preferred_element_type=jnp.float32,
    )
    first = lax.axis_index("row") * (plan.cols * plan.chunk)
    row_class = first + lax.broadcasted_iota(jnp.int32, change.shape, 0)
    return jnp.where(row_class < plan.classes, change, 0.0)


def spread_task(plan, change):
    done = []
    whole = yield from gather(change, [plan.wide] + plan.col_rest, done)
    return natural(whole, done, 0, None).reshape(plan.cols, -1, plan.per_col)


def return_task(plan, change):
    power = scale_of(change, 0)
    extra = jnp.broadcast_to(power.astype(jnp.int16), (16, plan.per_col))
    codes = jnp.concatenate([rounded(change, power), extra], axis=0)
    done = []
    codes = yield from gather(codes, plan.gather_order, done)
    codes = natural(codes, done, 0, None).reshape(plan.rows, -1, plan.per_col)
    change = restored(codes[:, :-16], codes[:, -16:][:, :1])
    return change.reshape(plan.padded, plan.per_col)[: plan.classes]


class Chain:
    def __init__(self, task, sizes):
        self.task, self.sizes = task, sizes
        self.value, self.ended, self.last = None, False, None
        self._send(None)

    def _send(self, value):
        try:
            self.asked = self.task.send(value)
        except StopIteration as end:
            self.value, self.ended = end.value, True

    def gate(self, *tokens):
        values = [v for v, _ in self.asked[0]]
        values, _ = lax.optimization_barrier((values, tokens))
        self.asked = ([(v, b) for v, (_, b) in zip(values, self.asked[0])],) + self.asked[1:]

    def advance(self, steps=None):
        while not self.ended and steps != 0:
            got = [swap(v, b, self.sizes) for v, b in self.asked[0]]
            self.last = got
            self._send((got, self.asked[1]))
            steps = steps - 1 if steps is not None else None
        return self.value


def on_device(sizes, points, targets, coeffs, block_inverse, block_order):
    plan = Plan(sizes, points.shape, targets.shape[2])
    blocks_here, per_col, block_size = plan.blocks_here, plan.per_col, plan.block_size
    my_row = lax.axis_index("row")
    my_col = lax.axis_index("col")
    ids = block_order[:STEPS]
    local = ids % blocks_here
    owners = ids // blocks_here
    turned = coeffs.transpose(0, 2, 1)
    wanted = targets.transpose(0, 2, 1)

    def place_of(s):
        first = jnp.where(my_row == owners[s], my_col * per_col, block_size)
        return jnp.stack([local[s], first]).astype(jnp.int32)

    def sum_of(s, active):
        return partial_sum(place_of(s), points, active, turned, wanted, plan.padded, 0, 1, None)

    codes = [inverse_codes(plan, pick(block_inverse, local[s], 0)) for s in range(STEPS)]
    spread = plan.row_bits
    near_done = 2 * spread - 1

    chains, actives, sums, reduces = [], [], [], []
    for s in range(STEPS):
        chains.append(Chain(points_task(plan, pick(points, local[s], 0), owners[s]), sizes))
        if s > 0:
            chains[s].gate(chains[s - 1].last)
        chains[s].advance(spread)
    inverse = Chain(inverse_task(plan, codes, owners), sizes)
    inverse.gate(chains[-1].last)
    inverse.advance(1)
    for s in range(STEPS):
        active = None
        if s > 0:
            chains[s].advance(near_done - spread + AHEAD - 1)
            chains[s].gate(sums[s - 1])
            active = chains[s].advance()
            reduces[s - 1].advance(1)
            active, _ = lax.optimization_barrier((active, reduces[s - 1].last))
        else:
            active = chains[s].advance()
            inverse.gate(active)
            inverse.advance(1)
        actives.append(active)
        sums.append(sum_of(s, active))
        reduces.append(Chain(reduce_task(plan, sums[s]), sizes))
    reduces[0].advance(1)
    reduces[0].gate(sums[-1])
    inverse.gate(sums[-1])
    while not reduces[-1].ended:
        reduces[-1].advance(1)
        for chain in (reduces[0], inverse):
            if not chain.ended:
                chain.advance(1)
                if not chain.ended and not reduces[-1].ended:
                    chain.gate(reduces[-1].last)
    inverses = inverse.advance()

    changes, spreads = [], []
    current = turned
    for s in range(STEPS):
        wrong = reduces[s].advance()
        for t in range(s):
            left, right = actives[t], actives[s]
            cross = kernel_of(left, squares_of(left), right, squares_of(right))
            wrong = wrong + lax.dot_general(
                spreads[t],
                cross.reshape(plan.cols, per_col, block_size),
                (((0, 2), (0, 1)), ((), ())),
                precision=HIGH,
                preferred_element_type=jnp.float32,
            )
        changes.append(change_of(plan, wrong, inverse_of(plan, inverses[s])))
        if s + 1 < STEPS:
            spreads.append(Chain(spread_task(plan, changes[s]), sizes).advance())
        change = Chain(return_task(plan, changes[s]), sizes).advance()
        previous = pick(current, local[s], 0)
        updated = jnp.where(my_row == owners[s], previous + change, previous)
        current = lax.dynamic_update_index_in_dim(current, updated, local[s], 0)
    return current.transpose(0, 2, 1)


def solution(mesh):
    sizes = dict(mesh.shape)
    placed = (
        P("row", "col", None),
        P("row", "col", None),
        P("row", "col", None),
        P("row", "col", None),
        P(),
    )

    def body(*args):
        return on_device(sizes, *args)

    return jax.shard_map(
        body, mesh=mesh, in_specs=placed, out_specs=P("row", "col", None), check_vma=False
    )
```
